256 devices in a mesh: row: 16 (over x_lo, z), col: 16 (over x_hi, y, core).
Axes of the slice: x: 4 (x_hi: 2, x_lo: 2; x = x_hi * 2 + x_lo), y: 4, z: 8, core: 2. Of those that a mesh axis runs over, the one named last changes fastest.
Arguments:
- ham_blocks: bfloat16 [128, 4, 128, 128], P('row'), may hold values from -0.25 to 0.25
- ham_index: int32 [128, 4], P('row'), may hold values from -1 to 127, as said below
- coef_blocks: bfloat16 [64, 16, 128, 128], P('col', 'row'), may hold values from -0.5 to 0.5
- coef_index: int32 [64, 16], P('col', 'row'), may hold values from 0 to 127, as said below
- slab_blocks: bfloat16 [16, 16, 128, 128], P('row', 'col'), may hold values from -0.5 to 0.5
- slab_index: int32 [16, 16], P('row', 'col'), may hold values from 0 to 127, as said below
- pattern_index: int32 [16, 32], P('row', 'col'), may hold values from 0 to 63, as said below
Outputs:
- reduced_blocks: bfloat16 [16, 32, 128, 128], P('row', 'col')
The draws below stay inside these ranges and needn't reach their ends.
Inputs may be any that keep to these rules, and one draw needn't show every extreme that they name: `ham_index`: each row lists its stored block columns first, all distinct, then -1 in every unused slot; a row holds 1 to 4 stored blocks, some row holds 4 and some row only one. `coef_index`: each row names 16 distinct orbital blocks. `slab_index`: each row names 16 distinct orbital blocks. `pattern_index`: entry k of a row names a block among (k // 2) * 4 to (k // 2) * 4 + 3.
All inputs are finite; a program needn't handle non-finite values.
Results may differ from the reference program's by a relative error of at most 0.0049.
Values may be sent and summed in bfloat16 or wider, within the bound.
No kernel may reach another device: no remote copies, remote signals or barrier semaphores. Data moves between devices by JAX's collectives and lax.ppermute only.
A program may use at most 128 MiB of HBM per device.

```python
import jax
import jax.numpy as jnp
from jax import lax

BLOCK = 128
HSTORE = 4
CSTORE = 16
OUTSTORE = 2
SFCOL_DEV = 4
PAO_BLOCKS = 128
SF_BLOCKS = 64
SLAB_BLOCKS = 16
OUT_STORED = 32


def distinct_rows(key, row_total, choices_total, picked_total):
    scores = jax.random.randint(key, (row_total, choices_total), 0, 1 << 20) * choices_total
    scores = scores + jnp.arange(choices_total, dtype=jnp.int32)[None, :]
    boost = jnp.zeros((row_total, choices_total), jnp.int32)
    boost = boost.at[0, 0].set(1 << 30).at[0, choices_total - 1].set(1 << 30)
    return lax.top_k(scores + boost, picked_total)[1].astype(jnp.int32)


def draw_ham_index(key, part):
    columns = distinct_rows(jax.random.fold_in(key, 11), PAO_BLOCKS, PAO_BLOCKS, HSTORE)
    counts = jax.random.randint(jax.random.fold_in(key, 12), (PAO_BLOCKS,), 1, HSTORE + 1)
    counts = counts.at[0].set(HSTORE).at[1].set(1)
    keep = jnp.arange(HSTORE, dtype=jnp.int32)[None, :] < counts[:, None]
    return jnp.where(keep, columns, -1).astype(jnp.int32)


def draw_coef_index(key, part):
    return distinct_rows(jax.random.fold_in(key, 13), SF_BLOCKS, PAO_BLOCKS, CSTORE)


def draw_slab_index(key, part):
    return distinct_rows(jax.random.fold_in(key, 14), SLAB_BLOCKS, PAO_BLOCKS, CSTORE)


def draw_pattern_index(key, part):
    groups = jnp.arange(OUT_STORED, dtype=jnp.int32) // OUTSTORE
    within = jax.random.randint(jax.random.fold_in(key, 15), (SLAB_BLOCKS, OUT_STORED), 0, SFCOL_DEV)
    within = within.at[0].set(SFCOL_DEV - 1).at[1].set(0)
    return (groups[None, :] * SFCOL_DEV + within).astype(jnp.int32)


def shard_levels(own_key, dims, pieces, smallest, largest):
    level = 1.0
    for position, parts in pieces:
        heights = jax.random.uniform(jax.random.fold_in(jax.random.fold_in(own_key, 6), position), (parts,), jnp.float32, smallest / len(pieces), largest / len(pieces))
        level = level * jnp.repeat(jnp.exp(heights), dims[position] // parts).reshape((-1,) + (1,) * (len(dims) - 1 - position))
    return level


def noise(stream_key, extent, scale, limit, split=(), kind=jnp.bfloat16):
    values = scale * jax.random.normal(stream_key, extent, jnp.float32)
    if split:
        values = values * shard_levels(stream_key, extent, split, -0.22, 0.18)
    return jnp.clip(values, -limit, limit).astype(kind)


def setup_inputs(seed: int = 0) -> dict:
    seeds = jax.random.split(jax.random.key(seed), 8)
    ham_blocks = noise(seeds[0], (PAO_BLOCKS, HSTORE, BLOCK, BLOCK), (HSTORE * BLOCK) ** -0.5, 0.25, ((0, 16),))
    ham_index = draw_ham_index(jax.random.fold_in(seeds[7], 71), 0)
    coef_blocks = noise(seeds[2], (SF_BLOCKS, CSTORE, BLOCK, BLOCK), BLOCK ** -0.5, 0.5, ((0, 16), (1, 16)))
    coef_index = draw_coef_index(jax.random.fold_in(seeds[7], 71), 0)
    slab_blocks = noise(seeds[4], (SLAB_BLOCKS, CSTORE, BLOCK, BLOCK), BLOCK ** -0.5, 0.5, ((0, 16), (1, 16)))
    slab_index = draw_slab_index(jax.random.fold_in(seeds[7], 71), 0)
    pattern_index = draw_pattern_index(jax.random.fold_in(seeds[7], 71), 0)
    return {"ham_blocks": ham_blocks, "ham_index": ham_index, "coef_blocks": coef_blocks, "coef_index": coef_index, "slab_blocks": slab_blocks, "slab_index": slab_index, "pattern_index": pattern_index}


def reference(ham_blocks, ham_index, coef_blocks, coef_index, slab_blocks, slab_index, pattern_index):
    owners = jnp.broadcast_to(jnp.arange(SF_BLOCKS, dtype=jnp.int32)[:, None], (SF_BLOCKS, CSTORE))
    transposed = jnp.zeros((PAO_BLOCKS, BLOCK, SF_BLOCKS, BLOCK), coef_blocks.dtype)
    transposed = transposed.at[coef_index, :, owners, :].set(jnp.swapaxes(coef_blocks, 2, 3))

    def row_image(row_item):
        block_row, index_row = row_item
        present = (index_row >= 0).astype(jnp.float32)
        gathered = transposed[jnp.maximum(index_row, 0)].astype(jnp.float32)
        masked = block_row.astype(jnp.float32) * present[:, None, None]
        return jnp.einsum("kxb,kbjc->xjc", masked, gathered).astype(jnp.bfloat16)

    images = lax.map(row_image, (ham_blocks, ham_index))

    def slab_row(row_item):
        coef_row, index_row, wanted = row_item
        needed = images[index_row][:, :, wanted, :].astype(jnp.float32)
        summed = jnp.einsum("mab,mbkc->akc", coef_row.astype(jnp.float32), needed)
        return jnp.transpose(summed, (1, 0, 2)).astype(jnp.bfloat16)

    return lax.map(slab_row, (slab_blocks, slab_index, pattern_index))
```

```python
import jax
import jax.numpy as jnp
from jax import lax
from jax.experimental import pallas as pl
from jax.experimental.pallas import tpu as pltpu
from jax.sharding import PartitionSpec as P


BF = jnp.bfloat16
F32 = jnp.float32
I32 = jnp.int32
ROWS, COLS = 16, 16
SHIFTS = ((1, 2), (1, 1), (1, 3), (0, 2), (1, 0), (0, 1), (0, 3))
SMEM = pl.BlockSpec(memory_space=pltpu.SMEM)
VMEM = pl.BlockSpec(memory_space=pltpu.VMEM)
ANY = pl.BlockSpec(memory_space=pl.ANY)


def iota(shape, dim):
    return lax.broadcasted_iota(I32, shape, dim)


def hot(cond):
    return jnp.where(cond, 1.0, 0.0).astype(BF)


def dot(a, b):
    return jnp.dot(a, b, preferred_element_type=F32)


def split_kernel(where, ham_idx, slab_idx, pattern, coef_idx, ham, coef, slab, send, own, swap, part, turned, sem):
    chip, core = where[1], where[2]
    copy = pltpu.make_async_copy(ham.at[:, :, pl.ds(pl.multiple_of(chip * 16, 16), 16), :], part, sem)
    copy.start()
    for j in range(4):
        turned[j] = coef[j, 0].T
    own[...] = turned[:, pl.ds(pl.multiple_of(core * 64, 64), 64), :]
    swap[0:256, :] = turned[:, pl.ds(pl.multiple_of((1 - core) * 64, 64), 64), :].reshape(256, 128)
    swap[256:384, :] = slab[0, 0]
    lane, line = iota((8, 128), 1), iota((8, 128), 0)
    meta = jnp.zeros((8, 128), I32)
    for p in range(8):
        for k in range(4):
            meta = jnp.where((line == p) & (lane == k), ham_idx[p, k], meta)
    meta = jnp.where(lane == 4, slab_idx[0, 0], meta)
    for e in range(2):
        meta = jnp.where(lane == 5 + e, pattern[0, e], meta)
    for j in range(4):
        meta = jnp.where(lane == 7 + j, coef_idx[j, 0], meta)
    send[:, :, 256:384] = jnp.broadcast_to(meta.astype(F32).astype(BF)[None], (16, 8, 128))
    a, b = iota((128, 128), 0), iota((128, 128), 1)
    order = hot((a // 8 == b % 16) & (a % 8 == b // 16))
    first = hot((b < 64) & (a == b + 64 * core))
    second = hot((b >= 64) & (a == b - 64 + 64 * core))
    copy.wait()
    for s in range(2):
        left = part[:, 2 * s].reshape(128, 128)
        right = part[:, 2 * s + 1].reshape(128, 128)
        half = (dot(left, first) + dot(right, second)).astype(BF)
        send[:, :, s * 128 : (s + 1) * 128] = dot(order, half).reshape(16, 8, 128).astype(BF)


def table_kernel(got, send):
    meta = got[:, :, 256:384].astype(F32).reshape(128, 128).astype(BF)
    a, b = iota((128, 128), 0), iota((128, 128), 1)
    picked = dot(meta, hot(a == 4 + b // 16))
    line = jnp.sum(jnp.where((a % 8 == 0) & (a // 8 == b % 16), picked, 0.0), axis=0, keepdims=True)
    send[...] = jnp.broadcast_to(line.reshape(1, 1, 128), (16, 8, 128)).astype(BF)


def pick_kernel(got, tables, send):
    pieces = got[:, :, 0:256].astype(F32).reshape(128, 256).astype(BF)
    flat = tables[...].astype(F32).reshape(128, 128).astype(BF)
    a, b = iota((16, 128), 0), iota((16, 128), 1)
    names = dot(hot(b == 8 * a), flat)
    lane = b.astype(F32)
    picks = jnp.concatenate([jnp.where(names[:, r : r + 1] == lane, 1.0, 0.0) for r in range(16)], axis=0)
    send[...] = dot(picks.astype(BF), pieces).astype(BF).reshape(16, 16, 256)


def pack_kernel(where, got, slab, swapped, piece):
    core = where[2]
    a, b = iota((256, 256), 0), iota((256, 256), 1)
    order = hot((a // 16 == b % 16) & (a % 16 == b // 16))
    piece[0:16] = dot(order, got[...].reshape(256, 256)).astype(BF).reshape(16, 16, 256)
    mine, other = slab[0, 0], swapped[256:384, :]
    low = jnp.where(core == 0, mine, other)
    high = jnp.where(core == 0, other, mine)
    piece[16:24, :, 0:128] = low.reshape(8, 16, 128)
    piece[16:24, :, 128:256] = high.reshape(8, 16, 128)


def choose_kernel(where, tables, own, swapped, send, both):
    chip, core = where[1], where[2]
    both[core] = own[...]
    both[1 - core] = swapped[0:256, :].reshape(4, 64, 128)
    for r in range(16):
        for i in range(4):
            col = 2 * chip + i // 2
            j = tables[col, 16 + 16 * (i % 2) + r] - 4 * col
            send[r, i] = both[i // 2, j]


def match_kernel(where, ham_names, tables, out, slots):
    row, chip = where[0], where[1]

    def clear(q, _):
        for i in range(4):
            slots[i * 128 + q] = -1
        return 0

    lax.fori_loop(0, 128, clear, 0)
    for i in range(4):
        col = 2 * chip + i // 2
        j = tables[col, 16 + 16 * (i % 2) + row] - 4 * col
        for m in range(16):
            slots[i * 128 + tables[col, 48 + j * 16 + m]] = m

    def one(m, _):
        p = tables[m, row]
        for k in range(4):
            q = ham_names[p, k]
            for i in range(4):
                out[m * 16 + k * 4 + i] = jnp.where(q >= 0, slots[i * 128 + jnp.maximum(q, 0)], -1)
        return 0

    lax.fori_loop(0, 16, one, 0)


def product_kernel(where, match, coefs, *refs):
    pieces, (own, send), (ham, slab, image, chosen, sems) = refs[:8], refs[8:10], refs[10:]
    chip, core = where[1], where[2]
    x, y = chip // 4, chip % 4
    copies = []
    for t, (dx, dy) in enumerate(((0, 0),) + SHIFTS):
        s = ((x + dx) % 2) * 4 + (y - dy + 4) % 4
        at = pl.ds(pl.multiple_of(s * 16, 16), 16)
        copies.append(pltpu.make_async_copy(pieces[t].at[0:16], ham.at[:, at, :], sems.at[2 * t]))
        copies.append(pltpu.make_async_copy(pieces[t].at[16:24], slab.at[s], sems.at[2 * t + 1]))
    for copy in copies:
        copy.start()

    for copy in copies:
        copy.wait()

    for m in range(16):
        for k in range(4):
            for i in range(4):
                slot = match[m * 16 + k * 4 + i]
                found = coefs[jnp.maximum(slot, 0), i]
                chosen[m % 2, k * 64 : k * 64 + 64, i * 128 : i * 128 + 128] = jnp.where(slot >= 0, found, jnp.zeros_like(found))
        image[m * 128 : m * 128 + 128, :] = dot(ham[m], chosen[m % 2]).astype(BF)
    total = jnp.zeros((128, 512), F32)
    for s in range(8):
        total = total + dot(slab[s].reshape(128, 256), image[s * 256 : s * 256 + 256, :])
    for e in range(2):
        low, high = total[:, e * 128 : e * 128 + 128], total[:, 256 + e * 128 : 384 + e * 128]
        own[e] = jnp.where(core == 0, low, high)
        send[e] = jnp.where(core == 0, high, low).astype(BF)


def shards(ham_blocks, ham_index, coef_blocks, coef_index, slab_blocks, slab_index, pattern_index):
    col = lax.axis_index("col")
    where = jnp.stack([lax.axis_index("row"), col // 2, col % 2]).astype(I32)
    cores = [(i, i ^ 1) for i in range(COLS)]
    sd = jax.ShapeDtypeStruct

    send, half, swap = pl.pallas_call(
        split_kernel,
        out_shape=(sd((16, 8, 384), BF), sd((4, 64, 128), BF), sd((384, 128), BF)),
        in_specs=[SMEM] * 5 + [ANY, VMEM, VMEM],
        out_specs=(VMEM,) * 3,
        scratch_shapes=[pltpu.VMEM((8, 4, 16, 128), BF), pltpu.VMEM((4, 128, 128), BF), pltpu.SemaphoreType.DMA],
        name="split",
    )(where, ham_index, slab_index, pattern_index, coef_index, ham_blocks, coef_blocks, slab_blocks)
    got = lax.all_to_all(send, "row", 0, 0)
    swapped = lax.ppermute(swap, "col", cores)

    named = pl.pallas_call(
        table_kernel, out_shape=sd((16, 8, 128), BF), in_specs=[VMEM], out_specs=VMEM, name="table"
    )(got)
    tables = lax.all_to_all(named, "col", 0, 0)

    picked = pl.pallas_call(
        pick_kernel, out_shape=sd((16, 16, 256), BF), in_specs=[VMEM] * 2, out_specs=VMEM, name="pick"
    )(got, tables)
    parts = lax.all_to_all(picked, "row", 0, 0)

    numbers = tables[:, 0, :].astype(I32)
    ham_names = got[:, :, 256:260].reshape(128, 4).astype(I32)
    wanted = pl.pallas_call(
        choose_kernel,
        out_shape=sd((16, 4, 64, 128), BF),
        in_specs=[SMEM, SMEM, VMEM, VMEM],
        out_specs=VMEM,
        scratch_shapes=[pltpu.VMEM((2, 4, 64, 128), BF)],
        name="choose",
    )(where, numbers, half, swapped)
    wanted, parts = lax.optimization_barrier((wanted, parts))
    coefs = lax.all_to_all(wanted, "row", 0, 0)

    piece = pl.pallas_call(
        pack_kernel, out_shape=sd((24, 16, 256), BF), in_specs=[SMEM] + [VMEM] * 3, out_specs=VMEM, name="pack"
    )(where, parts, slab_blocks, swapped)
    pieces = [piece]
    for dx, dy in SHIFTS:
        pairs = [
            (x * 8 + y * 2 + k, ((x + dx) % 2) * 8 + ((y + dy) % 4) * 2 + k)
            for x in range(2)
            for y in range(4)
            for k in range(2)
        ]
        pieces.append(lax.ppermute(piece, "col", pairs))

    match = pl.pallas_call(
        match_kernel,
        out_shape=sd((256,), I32),
        in_specs=[SMEM] * 3,
        out_specs=SMEM,
        scratch_shapes=[pltpu.SMEM((512,), I32)],
        name="match",
    )(where, ham_names, numbers)

    mine, other = pl.pallas_call(
        product_kernel,
        out_shape=(sd((2, 128, 128), F32), sd((2, 128, 128), BF)),
        in_specs=[SMEM, SMEM, VMEM] + [ANY] * 8,
        out_specs=(VMEM, VMEM),
        scratch_shapes=[
            pltpu.VMEM((16, 128, 256), BF),
            pltpu.VMEM((8, 8, 16, 256), BF),
            pltpu.VMEM((2048, 512), BF),
            pltpu.VMEM((2, 256, 512), BF),
            pltpu.SemaphoreType.DMA((16,)),
        ],
        name="product",
    )(where, match, coefs, *pieces)
    theirs = lax.ppermute(other, "col", cores)
    return (mine + theirs.astype(F32)).astype(BF)[None]


def solution(mesh):
    placed = (
        P("row", None, None, None),
        P("row", None),
        P("col", "row", None, None),
        P("col", "row"),
        P("row", "col", None, None),
        P("row", "col"),
        P("row", "col"),
    )
    return jax.shard_map(
        shards, mesh=mesh, in_specs=placed, out_specs=P("row", "col", None, None), check_vma=False
    )
```

```python
import jax
import jax.numpy as jnp
from jax import lax
from jax.experimental import pallas as pl
from jax.experimental.pallas import tpu as pltpu
from jax.sharding import PartitionSpec as P


BF = jnp.bfloat16
F32 = jnp.float32
I32 = jnp.int32
COLS = 16
PLACES = ((0, 0), (1, 0), (0, 1), (1, 1), (0, 3), (1, 3), (0, 2), (1, 2))
SMEM = pl.BlockSpec(memory_space=pltpu.SMEM)
VMEM = pl.BlockSpec(memory_space=pltpu.VMEM)
ANY = pl.BlockSpec(memory_space=pl.ANY)


def iota(shape, dim):
    return lax.broadcasted_iota(I32, shape, dim)


def hot(cond):
    return jnp.where(cond, 1.0, 0.0).astype(BF)


def dot(a, b):
    return jnp.dot(a, b, preferred_element_type=F32)


def split_kernel(coef_idx, ham, coef, slab, send, own, swap, part, turned, sem):
    col = lax.axis_index("col")
    chip, core = col // 2, col % 2
    copy = pltpu.make_async_copy(ham.at[:, :, pl.ds(pl.multiple_of(chip * 16, 16), 16), :], part, sem)
    copy.start()
    for j in range(4):
        turned[j] = coef[j, 0].T
    own[...] = turned[:, pl.ds(pl.multiple_of(core * 64, 64), 64), :]
    swap[0:256, :] = turned[:, pl.ds(pl.multiple_of((1 - core) * 64, 64), 64), :].reshape(256, 128)
    swap[256:384, :] = slab[0, 0]
    lane = iota((16, 128), 1)
    names = jnp.zeros((16, 128), I32)
    for j in range(4):
        names = jnp.where(lane == j, coef_idx[j, 0], names)
    swap[384:400, :] = names.astype(F32).astype(BF)
    a, b = iota((128, 128), 0), iota((128, 128), 1)
    order = hot((a // 8 == b % 16) & (a % 8 == b // 16))
    first = hot((b < 64) & (a == b + 64 * core))
    second = hot((b >= 64) & (a == b - 64 + 64 * core))
    copy.wait()
    for s in range(2):
        left = part[:, 2 * s].reshape(128, 128)
        right = part[:, 2 * s + 1].reshape(128, 128)
        half = (dot(left, first) + dot(right, second)).astype(BF)
        send[:, :, s * 128 : (s + 1) * 128] = dot(order, half).reshape(16, 8, 128).astype(BF)


def stamp_kernel(ham_idx, coef_idx, named, swapped, parts, send):
    send[:, :, 0:256] = parts[...]
    lane, line = iota((8, 128), 1), iota((8, 128), 0)
    meta = jnp.zeros((8, 128), I32)
    for p in range(8):
        for k in range(4):
            meta = jnp.where((line == p) & (lane == k), ham_idx[p, k], meta)
    for j in range(4):
        meta = jnp.where(lane == 4 + j, coef_idx[j, 0], meta)
    a, b = iota((128, 128), 0), iota((128, 128), 1)
    flat = named[...].astype(F32).reshape(128, 128).astype(BF)
    slabs = (b >= 16) & (b < 32)
    pats = (b >= 32) & (b < 64)
    src = jnp.where(slabs, 0, 1 + b % 2)
    at = jnp.where(slabs, b - 16, (b - 32) // 2)
    picked = dot(flat, hot((slabs | pats) & (a == src)))
    line_all = jnp.sum(jnp.where(a == 8 * at, picked, 0.0), axis=0, keepdims=True)
    others = dot(swapped[384:400, :], hot((b >= 8) & (b < 12) & (a == b - 8)))[0:8]
    meta = meta.astype(F32) + line_all + others
    send[:, :, 256:384] = jnp.broadcast_to(meta.astype(BF)[None], (16, 8, 128))


def pick_kernel(got, send):
    pieces = got[:, :, 0:256].astype(F32).reshape(128, 256).astype(BF)
    flat = got[:, :, 256:384].astype(F32).reshape(128, 128).astype(BF)
    a, b = iota((16, 128), 0), iota((16, 128), 1)
    names = lax.dot_general(hot(b == 16 + a), flat, (((1,), (1,)), ((), ())), preferred_element_type=F32)
    lane = b.astype(F32)
    picks = jnp.concatenate(
        [jnp.where(names[:, 8 * r : 8 * r + 1] == lane, 1.0, 0.0) for r in range(16)], axis=0
    )
    send[...] = dot(picks.astype(BF), pieces).astype(BF).reshape(16, 16, 256)


def pack_kernel(got, piece):
    a, b = iota((256, 256), 0), iota((256, 256), 1)
    order = hot((a // 16 == b % 16) & (a % 16 == b // 16))
    piece[...] = dot(order, got[...].reshape(256, 256)).astype(BF).reshape(16, 16, 256)


def choose_kernel(tables, own, swapped, send, both):
    col = lax.axis_index("col")
    chip, core = col // 2, col % 2
    both[core] = own[...]
    both[1 - core] = swapped[0:256, :].reshape(4, 64, 128)
    for r in range(16):
        for i in range(4):
            at = 2 * chip + i // 2
            j = tables[r, 32 + 2 * at + i % 2] - 4 * at
            send[r, i] = both[i // 2, j]


def match_kernel(ham_names, tables, out, slots):
    row, col = lax.axis_index("row"), lax.axis_index("col")
    chip, core = col // 2, col % 2

    def clear(q, _):
        for i in range(4):
            slots[i * 128 + q] = -1
        return 0

    lax.fori_loop(0, 128, clear, 0)
    for i in range(4):
        at = 2 * chip + i // 2
        j = tables[row, 32 + 2 * at + i % 2] - 4 * at
        base = jnp.where(core == i // 2, 4, 8) + j
        for m in range(16):
            slots[i * 128 + tables[m, base]] = m

    def one(m, _):
        p = tables[row, 16 + m]
        for k in range(4):
            q = ham_names[p, k]
            for i in range(4):
                out[m * 16 + k * 4 + i] = jnp.where(q >= 0, slots[i * 128 + jnp.maximum(q, 0)], -1)
        return 0

    lax.fori_loop(0, 16, one, 0)


def product_kernel(match, coefs, *refs):
    hams, slabs, (own, send), (ham, slab, image, chosen, sems) = refs[:8], refs[8:12], refs[12:14], refs[14:]
    col = lax.axis_index("col")
    chip, core = col // 2, col % 2
    x, y = chip // 4, chip % 4
    copies = []
    for t, (dx, dy) in enumerate(PLACES):
        s = ((x + dx) % 2) * 4 + (y - dy + 4) % 4
        at = pl.ds(pl.multiple_of(s * 16, 16), 16)
        copies.append(pltpu.make_async_copy(hams[t], ham.at[:, at, :], sems.at[t]))
        if t % 2 == 0:
            for h in range(2):
                s = ((x + h) % 2) * 4 + (y - dy + 4) % 4
                copies.append(pltpu.make_async_copy(slabs[t // 2].at[h], slab.at[s], sems.at[8 + t + h]))
    for copy in copies:
        copy.start()
    for copy in copies:
        copy.wait()

    total = jnp.zeros((128, 512), F32)
    for s in range(8):
        for h in range(2):
            m = 2 * s + (core + h) % 2
            for k in range(4):
                for i in range(4):
                    slot = match[m * 16 + k * 4 + i]
                    found = coefs[jnp.maximum(slot, 0), i]
                    chosen[h, k * 64 : k * 64 + 64, i * 128 : i * 128 + 128] = jnp.where(slot >= 0, found, jnp.zeros_like(found))
            image[s, h * 128 : h * 128 + 128, :] = dot(ham[m], chosen[h]).astype(BF)
    for s in range(8):
        for h in range(2):
            total = total + dot(slab[s, h], image[s, h * 128 : h * 128 + 128, :])
    for e in range(2):
        low, high = total[:, e * 128 : e * 128 + 128], total[:, 256 + e * 128 : 384 + e * 128]
        own[e] = jnp.where(core == 0, low, high)
        send[e] = jnp.where(core == 0, high, low).astype(BF)


def shift(value, dx, dy):
    pairs = [
        (x * 8 + y * 2 + k, ((x + dx) % 2) * 8 + ((y + dy) % 4) * 2 + k)
        for x in range(2)
        for y in range(4)
        for k in range(2)
    ]
    return lax.ppermute(value, "col", pairs)


def near(value):
    return pltpu.with_memory_space_constraint(value, pltpu.VMEM)


def run(kernel, outs, specs, args, scratch=()):
    args = [near(v) if spec == "near" else v for spec, v in zip(specs, args)]
    specs = [VMEM if spec == "near" else spec for spec in specs]
    single = not isinstance(outs, list)
    outs = [outs] if single else outs
    result = pl.pallas_call(
        kernel,
        out_shape=[pltpu.VMEM(shape, kind) for shape, kind in outs],
        in_specs=specs,
        out_specs=[VMEM] * len(outs),
        scratch_shapes=scratch,
    )(*args)
    return result[0] if single else result


def body(ham_blocks, ham_index, coef_blocks, coef_index, slab_blocks, slab_index, pattern_index):
    cores = [(i, i ^ 1) for i in range(COLS)]

    names = jnp.concatenate([slab_index, pattern_index], axis=1).astype(BF)
    names = jnp.broadcast_to(jnp.pad(names, ((0, 7), (0, 125)))[None], (COLS, 8, 128))
    named = lax.all_to_all(names, "col", 0, 0)

    parts, half, swap = run(
        split_kernel,
        [((16, 8, 256), BF), ((4, 64, 128), BF), ((400, 128), BF)],
        [SMEM, ANY, VMEM, VMEM],
        [coef_index, ham_blocks, coef_blocks, slab_blocks],
        [pltpu.VMEM((8, 4, 16, 128), BF), pltpu.VMEM((4, 128, 128), BF), pltpu.SemaphoreType.DMA],
    )
    swapped = lax.ppermute(swap, "col", cores)

    stamped = run(
        stamp_kernel,
        ((16, 8, 384), BF),
        [SMEM, SMEM, "near", "near", "near"],
        [ham_index, coef_index, named, swapped, parts],
    )
    got = lax.all_to_all(stamped, "row", 0, 0)

    pair = jnp.stack([slab_blocks[0, 0], swapped[256:384]]).reshape(2, 128, 128)
    quad = jnp.stack([pair, shift(pair, 1, 0)])
    quads = [quad] + [shift(quad, 0, d) for d in (1, 3, 2)]

    picked = run(pick_kernel, ((16, 16, 256), BF), ["near"], [got])
    picks = lax.all_to_all(picked, "row", 0, 0)

    numbers = got[:, 0, 256:384].astype(I32)
    ham_names = got[:, :, 256:260].reshape(128, 4).astype(I32)
    wanted = run(
        choose_kernel,
        ((16, 4, 64, 128), BF),
        [SMEM, "near", "near"],
        [numbers, half, swapped],
        [pltpu.VMEM((2, 4, 64, 128), BF)],
    )
    wanted, picks, *quads = lax.optimization_barrier((wanted, picks, *quads))
    coefs = lax.all_to_all(wanted, "row", 0, 0)

    piece = run(pack_kernel, ((16, 16, 256), BF), ["near"], [picks])
    across = shift(piece, 1, 0)
    hams = [piece, across]
    for d in (1, 3, 2):
        hams += [shift(piece, 0, d), shift(across, 0, d)]

    match = pl.pallas_call(
        match_kernel,
        out_shape=jax.ShapeDtypeStruct((256,), I32),
        in_specs=[SMEM] * 2,
        out_specs=SMEM,
        scratch_shapes=[pltpu.SMEM((512,), I32)],
        name="match",
    )(ham_names, numbers)

    mine, other = run(
        product_kernel,
        [((2, 128, 128), F32), ((2, 128, 128), BF)],
        [SMEM] + ["near"] * 13,
        [match, coefs, *hams, *quads],
        [
            pltpu.VMEM((16, 128, 256), BF),
            pltpu.VMEM((8, 2, 128, 128), BF),
            pltpu.VMEM((8, 256, 512), BF),
            pltpu.VMEM((2, 256, 512), BF),
            pltpu.SemaphoreType.DMA((16,)),
        ],
    )
    theirs = lax.ppermute(other, "col", cores)
    return (mine + theirs.astype(F32)).astype(BF)[None]


def solution(mesh):
    placed = (
        P("row", None, None, None),
        P("row", None),
        P("col", "row", None, None),
        P("col", "row"),
        P("row", "col", None, None),
        P("row", "col"),
        P("row", "col"),
    )
    return jax.shard_map(
        body, mesh=mesh, in_specs=placed, out_specs=P("row", "col", None, None), check_vma=False
    )
```

```python
import functools

import jax
import jax.numpy as jnp
from jax import lax
from jax.experimental import pallas as pl
from jax.experimental.pallas import tpu as pltpu
from jax.sharding import PartitionSpec as P


BF = jnp.bfloat16
F32 = jnp.float32
I32 = jnp.int32
COLS = 16
PLACES = ((0, 0), (1, 0), (0, 1), (1, 1), (0, 3), (1, 3), (0, 2), (1, 2))
SMEM = pl.BlockSpec(memory_space=pltpu.SMEM)
VMEM = pl.BlockSpec(memory_space=pltpu.VMEM)
ANY = pl.BlockSpec(memory_space=pl.ANY)


def iota(shape, dim):
    return lax.broadcasted_iota(I32, shape, dim)


def hot(cond):
    return jnp.where(cond, 1.0, 0.0).astype(BF)


def dot(a, b):
    return jnp.dot(a, b, preferred_element_type=F32)


def name_kernel(slab_idx, pattern, send):
    lane = iota((8, 128), 1)
    line = jnp.where(lane == 0, slab_idx[0, 0], jnp.where(lane == 1, pattern[0, 0], pattern[0, 1]))
    send[...] = jnp.broadcast_to(line.astype(F32).astype(BF)[None], send.shape)


def split_kernel(coef_idx, ham, coef, slab, send, own, swap, part, turned, sem):
    col = lax.axis_index("col")
    chip, core = col // 2, col % 2
    copy = pltpu.make_async_copy(ham.at[:, :, pl.ds(pl.multiple_of(chip * 16, 16), 16), :], part, sem)
    copy.start()
    for j in range(4):
        turned[j] = coef[j, 0].T
    own[...] = turned[:, pl.ds(pl.multiple_of(core * 64, 64), 64), :]
    swap[0:256, :] = turned[:, pl.ds(pl.multiple_of((1 - core) * 64, 64), 64), :].reshape(256, 128)
    swap[256:384, :] = slab[0, 0]
    lane = iota((16, 128), 1)
    names = jnp.zeros((16, 128), I32)
    for j in range(4):
        names = jnp.where(lane == j, coef_idx[j, 0], names)
    swap[384:400, :] = names.astype(F32).astype(BF)
    a, b = iota((128, 128), 0), iota((128, 128), 1)
    order = hot((a // 8 == b % 16) & (a % 8 == b // 16))
    first = hot((b < 64) & (a == b + 64 * core))
    second = hot((b >= 64) & (a == b - 64 + 64 * core))
    copy.wait()
    for s in range(2):
        left = part[:, 2 * s].reshape(128, 128)
        right = part[:, 2 * s + 1].reshape(128, 128)
        half = (dot(left, first) + dot(right, second)).astype(BF)
        send[:, :, s * 128 : (s + 1) * 128] = dot(order, half).reshape(16, 8, 128).astype(BF)


def stamp_kernel(ham_idx, coef_idx, named, swapped, parts, send):
    send[:, :, 0:256] = parts[...]
    lane, line = iota((8, 128), 1), iota((8, 128), 0)
    meta = jnp.zeros((8, 128), I32)
    for p in range(8):
        for k in range(4):
            meta = jnp.where((line == p) & (lane == k), ham_idx[p, k], meta)
    for j in range(4):
        meta = jnp.where(lane == 4 + j, coef_idx[j, 0], meta)
    a, b = iota((128, 128), 0), iota((128, 128), 1)
    flat = named[...].astype(F32).reshape(128, 128).astype(BF)
    slabs = (b >= 16) & (b < 32)
    pats = (b >= 32) & (b < 64)
    src = jnp.where(slabs, 0, 1 + b % 2)
    at = jnp.where(slabs, b - 16, (b - 32) // 2)
    picked = dot(flat, hot((slabs | pats) & (a == src)))
    line_all = jnp.sum(jnp.where(a == 8 * at, picked, 0.0), axis=0, keepdims=True)
    others = dot(swapped[384:400, :], hot((b >= 8) & (b < 12) & (a == b - 8)))[0:8]
    meta = meta.astype(F32) + line_all + others
    send[:, :, 256:384] = jnp.broadcast_to(meta.astype(BF)[None], (16, 8, 128))


def pick_kernel(got, send):
    pieces = got[:, :, 0:256].astype(F32).reshape(128, 256).astype(BF)
    flat = got[:, :, 256:384].astype(F32).reshape(128, 128).astype(BF)
    a, b = iota((16, 128), 0), iota((16, 128), 1)
    names = lax.dot_general(hot(b == 16 + a), flat, (((1,), (1,)), ((), ())), preferred_element_type=F32)
    lane = b.astype(F32)
    picks = jnp.concatenate(
        [jnp.where(names[:, 8 * r : 8 * r + 1] == lane, 1.0, 0.0) for r in range(16)], axis=0
    )
    send[...] = dot(picks.astype(BF), pieces).astype(BF).reshape(16, 16, 256)


def pack_kernel(got, piece):
    a, b = iota((256, 256), 0), iota((256, 256), 1)
    order = hot((a // 16 == b % 16) & (a % 16 == b // 16))
    piece[...] = dot(order, got[...].reshape(256, 256)).astype(BF).reshape(16, 16, 256)


def choose_kernel(tables, own, swapped, send, both):
    col = lax.axis_index("col")
    chip, core = col // 2, col % 2
    both[core] = own[...]
    both[1 - core] = swapped[0:256, :].reshape(4, 64, 128)
    for r in range(16):
        for i in range(4):
            at = 2 * chip + i // 2
            j = tables[r, 32 + 2 * at + i % 2] - 4 * at
            send[r, 64 * i : 64 * i + 64] = both[i // 2, j]


def match_kernel(ham_names, tables, out, slots):
    row, col = lax.axis_index("row"), lax.axis_index("col")
    chip, core = col // 2, col % 2

    def clear(q, _):
        for i in range(64):
            slots[q * 64 + i] = -1
        return 0

    lax.fori_loop(0, 8, clear, 0)
    for i in range(4):
        at = 2 * chip + i // 2
        j = tables[row, 32 + 2 * at + i % 2] - 4 * at
        base = jnp.where(core == i // 2, 4, 8) + j
        for m in range(16):
            slots[i * 128 + tables[m, base]] = m

    for m in range(16):
        p = tables[row, 16 + m]
        for k in range(4):
            q = ham_names[p, k]
            for i in range(4):
                out[m * 16 + k * 4 + i] = jnp.where(q >= 0, slots[i * 128 + jnp.maximum(q, 0)], -1)


def gather_kernel(*refs):
    hams, slabs, (ham, slab) = refs[:8], refs[8:10], refs[10:]
    col = lax.axis_index("col")
    chip, core = col // 2, col % 2
    x, y = chip // 4, chip % 4
    for t, (dx, dy) in enumerate(PLACES):
        s = ((x + dx) % 2) * 4 + (y - dy + 4) % 4
        ham[:, pl.ds(pl.multiple_of(s * 16, 16), 16), :] = hams[t][...]
        for h in range(2):
            slab[2 * s + (core + h) % 2] = slabs[dx][t // 2, h]


def product_kernel(mine, match, coefs, ham, slab, out, image, chosen):
    core = lax.axis_index("col") % 2
    pair = core if mine else 1 - core
    total = jnp.zeros((128, 256), F32)
    for m in range(16):
        for k in range(4):
            for e in range(2):
                slot = match[m * 16 + k * 4 + 2 * pair + e]
                at = pl.ds(pl.multiple_of(128 * pair + 64 * e, 64), 64)
                found = coefs[jnp.maximum(slot, 0), at]
                chosen[m % 4, k * 64 : k * 64 + 64, e * 128 : e * 128 + 128] = jnp.where(
                    slot >= 0, found, jnp.zeros_like(found)
                )
        image[m] = dot(ham[m], chosen[m % 4]).astype(BF)
    for m in range(16):
        total = total + dot(slab[m], image[m])
    for e in range(2):
        out[e] = total[:, e * 128 : e * 128 + 128].astype(out.dtype)


def shift(value, dx, dy):
    pairs = [
        (x * 8 + y * 2 + k, ((x + dx) % 2) * 8 + ((y + dy) % 4) * 2 + k)
        for x in range(2)
        for y in range(4)
        for k in range(2)
    ]
    return lax.ppermute(value, "col", pairs)


def near(value):
    return pltpu.with_memory_space_constraint(value, pltpu.VMEM)


def run(kernel, outs, specs, args, scratch=(), limit=None):
    args = [near(v) if spec == "near" else v for spec, v in zip(specs, args)]
    specs = [VMEM if spec == "near" else spec for spec in specs]
    single = not isinstance(outs, list)
    outs = [outs] if single else outs
    result = pl.pallas_call(
        kernel,
        out_shape=[pltpu.VMEM(shape, kind) for shape, kind in outs],
        in_specs=specs,
        out_specs=[VMEM] * len(outs),
        scratch_shapes=scratch,
        compiler_params=pltpu.CompilerParams(vmem_limit_bytes=limit),
    )(*args)
    return result[0] if single else result


def body(ham_blocks, ham_index, coef_blocks, coef_index, slab_blocks, slab_index, pattern_index):
    cores = [(i, i ^ 1) for i in range(COLS)]

    names = run(name_kernel, ((COLS, 8, 128), BF), [SMEM, SMEM], [slab_index, pattern_index])
    named = lax.all_to_all(names, "col", 0, 0)

    parts, half, swap = run(
        split_kernel,
        [((16, 8, 256), BF), ((4, 64, 128), BF), ((400, 128), BF)],
        [SMEM, ANY, VMEM, VMEM],
        [coef_index, ham_blocks, coef_blocks, slab_blocks],
        [pltpu.VMEM((8, 4, 16, 128), BF), pltpu.VMEM((4, 128, 128), BF), pltpu.SemaphoreType.DMA],
    )
    swapped = lax.ppermute(swap, "col", cores)

    stamped = run(
        stamp_kernel,
        ((16, 8, 384), BF),
        [SMEM, SMEM, "near", "near", "near"],
        [ham_index, coef_index, named, swapped, parts],
    )
    got = lax.all_to_all(stamped, "row", 0, 0)

    pair = jnp.stack([slab_blocks[0, 0], swapped[256:384]]).reshape(2, 128, 128)
    line = [pair] + [shift(pair, 0, d) for d in (1, 3, 2)]
    line = jnp.stack(line)
    slabs = [line, shift(line, 1, 0)]

    picked = run(pick_kernel, ((16, 16, 256), BF), ["near"], [got])
    picks = lax.all_to_all(picked, "row", 0, 0)

    numbers = got[:, 0, 256:384].astype(I32)
    ham_names = got[:, :, 256:260].reshape(128, 4).astype(I32)
    wanted = run(
        choose_kernel,
        ((16, 256, 128), BF),
        [SMEM, "near", "near"],
        [numbers, half, swapped],
        [pltpu.VMEM((2, 4, 64, 128), BF)],
    )
    wanted, picks = lax.optimization_barrier((wanted, picks))
    coefs = lax.all_to_all(wanted, "row", 0, 0)

    piece = run(pack_kernel, ((16, 16, 256), BF), ["near"], [picks])
    across = shift(piece, 1, 0)
    hams = [piece, across]
    for d in (1, 3, 2):
        hams += [shift(piece, 0, d), shift(across, 0, d)]

    match = pl.pallas_call(
        match_kernel,
        out_shape=pltpu.SMEM((256,), I32),
        in_specs=[SMEM] * 2,
        out_specs=SMEM,
        scratch_shapes=[pltpu.SMEM((512,), I32)],
        name="match",
    )(ham_names, numbers)
    match = pltpu.with_memory_space_constraint(match, pltpu.SMEM)

    ham, slab = run(
        gather_kernel,
        [((16, 128, 256), BF), ((16, 128, 128), BF)],
        ["near"] * 10,
        [*hams, *slabs],
        limit=24 << 20,
    )

    def product(mine, kind):
        return run(
            functools.partial(product_kernel, mine),
            ((2, 128, 128), kind),
            [SMEM] + ["near"] * 3,
            [match, coefs, ham, slab],
            [pltpu.VMEM((16, 128, 256), BF), pltpu.VMEM((4, 256, 256), BF)],
            24 << 20,
        )

    other = product(False, BF)
    theirs = lax.ppermute(other, "col", cores)
    mine = product(True, F32)
    return (mine + theirs.astype(F32)).astype(BF)[None]


def solution(mesh):
    placed = (
        P("row", None, None, None),
        P("row", None),
        P("col", "row", None, None),
        P("col", "row"),
        P("row", "col", None, None),
        P("row", "col"),
        P("row", "col"),
    )
    return jax.shard_map(
        body, mesh=mesh, in_specs=placed, out_specs=P("row", "col", None, None), check_vma=False
    )
```

```python
import jax
import jax.numpy as jnp
from jax import lax
from jax.experimental import pallas as pl
from jax.experimental.pallas import tpu as pltpu
from jax.sharding import PartitionSpec as P


BF = jnp.bfloat16
F32 = jnp.float32
I32 = jnp.int32
COLS = 16
LIMIT = 16 << 20
PLACES = ((0, 0), (1, 0), (0, 1), (1, 1), (0, 3), (1, 3), (0, 2), (1, 2))
SMEM = pl.BlockSpec(memory_space=pltpu.SMEM)
VMEM = pl.BlockSpec(memory_space=pltpu.VMEM)
ANY = pl.BlockSpec(memory_space=pl.ANY)


def iota(shape, dim):
    return lax.broadcasted_iota(I32, shape, dim)


def hot(cond):
    return jnp.where(cond, 1.0, 0.0).astype(BF)


def dot(a, b):
    return jnp.dot(a, b, preferred_element_type=F32)


def name_kernel(slab_idx, pattern, send):
    lane = iota((8, 128), 1)
    line = jnp.where(lane == 0, slab_idx[0:1, 0:1], jnp.where(lane == 1, pattern[0:1, 0:1], pattern[0:1, 1:2]))
    send[...] = jnp.broadcast_to(line.astype(F32).astype(BF)[None], send.shape)


def split_kernel(ham, coef, send, turned, part, sem):
    col = lax.axis_index("col")
    chip, core = col // 2, col % 2
    copy = pltpu.make_async_copy(ham.at[:, :, pl.ds(pl.multiple_of(chip * 16, 16), 16), :], part, sem)
    copy.start()
    for j in range(4):
        turned[j] = coef[j, 0].T
    a, b = iota((128, 128), 0), iota((128, 128), 1)
    order = hot((a // 8 == b % 16) & (a % 8 == b // 16))
    first = hot((b < 64) & (a == b + 64 * core))
    second = hot((b >= 64) & (a == b - 64 + 64 * core))
    copy.wait()
    for s in range(2):
        left = part[:, 2 * s].reshape(128, 128)
        right = part[:, 2 * s + 1].reshape(128, 128)
        half = (dot(left, first) + dot(right, second)).astype(BF)
        send[:, :, s * 128 : (s + 1) * 128] = dot(order, half).reshape(16, 8, 128).astype(BF)


def stamp_kernel(ham_idx, coef_idx, named, parts, send):
    send[:, :, 0:256] = parts[...]
    lane, line = iota((8, 128), 1), iota((8, 128), 0)
    meta = jnp.zeros((8, 128), I32)
    for p in range(8):
        for k in range(4):
            meta = jnp.where((line == p) & (lane == k), ham_idx[p, k], meta)
    for j in range(4):
        meta = jnp.where(lane == 4 + j, coef_idx[j, 0], meta)
    a, b = iota((128, 128), 0), iota((128, 128), 1)
    flat = named[...].astype(F32).reshape(128, 128).astype(BF)
    slabs = (b >= 16) & (b < 32)
    pats = (b >= 32) & (b < 64)
    src = jnp.where(slabs, 0, 1 + b % 2)
    at = jnp.where(slabs, b - 16, (b - 32) // 2)
    picked = dot(flat, hot((slabs | pats) & (a == src)))
    line_all = jnp.sum(jnp.where(a == 8 * at, picked, 0.0), axis=0, keepdims=True)
    meta = meta.astype(F32) + line_all
    send[:, :, 256:384] = jnp.broadcast_to(meta.astype(BF)[None], (16, 8, 128))


def pick_kernel(got, send):
    pieces = got[:, :, 0:256].astype(F32).reshape(128, 256).astype(BF)
    flat = got[:, :, 256:384].astype(F32).reshape(128, 128).astype(BF)
    a, b = iota((16, 128), 0), iota((16, 128), 1)
    names = lax.dot_general(hot(b == 16 + a), flat, (((1,), (1,)), ((), ())), preferred_element_type=F32)
    lane = b.astype(F32)
    picks = jnp.concatenate(
        [jnp.where(names[:, 8 * r : 8 * r + 1] == lane, 1.0, 0.0) for r in range(16)], axis=0
    )
    send[...] = dot(picks.astype(BF), pieces).astype(BF).reshape(16, 16, 256)


def pack_kernel(got, piece):
    a, b = iota((256, 256), 0), iota((256, 256), 1)
    order = hot((a // 16 == b % 16) & (a % 16 == b // 16))
    piece[...] = dot(order, got[...].reshape(256, 256)).astype(BF).reshape(16, 16, 256)


def choose_kernel(tables, turned, send):
    col = lax.axis_index("col")
    for r in range(16):
        for e in range(2):
            send[r, 128 * e : 128 * e + 128] = turned[tables[r, 32 + 2 * col + e] - 4 * col]


def match_kernel(ham_names, tables, out, slots):
    row, col = lax.axis_index("row"), lax.axis_index("col")

    def clear(q, _):
        for i in range(32):
            slots[q * 32 + i] = -1
        return 0

    lax.fori_loop(0, 8, clear, 0)
    for e in range(2):
        base = 4 + tables[row, 32 + 2 * col + e] - 4 * col
        for m in range(16):
            slots[e * 128 + tables[m, base]] = m
    for m in range(16):
        p = tables[row, 16 + m]
        for k in range(4):
            q = ham_names[p, k]
            for e in range(2):
                out[m * 8 + k * 2 + e] = jnp.where(q >= 0, slots[e * 128 + jnp.maximum(q, 0)], -1)


def gather_kernel(*refs):
    hams, ham = refs[:8], refs[8]
    chip = lax.axis_index("col") // 2
    x, y = chip // 4, chip % 4
    for t, (dx, dy) in enumerate(PLACES):
        s = ((x + dx) % 2) * 4 + (y - dy + 4) % 4
        ham[:, pl.ds(pl.multiple_of(s * 16, 16), 16), :] = hams[t][...]


def product_kernel(match, coefs, ham, across, near_slabs, far_slabs, out, image, chosen):
    col = lax.axis_index("col")
    chip, core = col // 2, col % 2
    x, y = chip // 4, chip % 4
    for m in range(16):
        for k in range(4):
            for e in range(2):
                slot = match[m * 8 + k * 2 + e]
                for h in range(2):
                    half = core if h == 0 else 1 - core
                    at = pl.ds(pl.multiple_of(128 * e + 64 * half, 64), 64)
                    found = coefs[jnp.maximum(slot, 0), at]
                    chosen[m % 2, h, k * 64 : k * 64 + 64, e * 128 : e * 128 + 128] = jnp.where(
                        slot >= 0, found, jnp.zeros_like(found)
                    )
        image[m // 2, 128 * (m % 2) : 128 * (m % 2) + 128] = (dot(ham[m], chosen[m % 2, 0]) + dot(across[m], chosen[m % 2, 1])).astype(BF)
    total = jnp.zeros((128, 256), F32)
    for s in range(8):
        d = (y - s % 4 + 4) % 4
        two = [jnp.where(x == s // 4, near_slabs[d, (h + core) % 2], far_slabs[d, (h + core) % 2]) for h in range(2)]
        total = total + dot(jnp.concatenate(two, axis=1), image[s])
    for e in range(2):
        out[0, e] = total[:, e * 128 : e * 128 + 128].astype(BF)


def shift(value, dx, dy):
    pairs = [
        (x * 8 + y * 2 + k, ((x + dx) % 2) * 8 + ((y + dy) % 4) * 2 + k)
        for x in range(2)
        for y in range(4)
        for k in range(2)
    ]
    return lax.ppermute(value, "col", pairs)


def near(value):
    return pltpu.with_memory_space_constraint(value, pltpu.VMEM)


def run(kernel, outs, specs, args, scratch=(), limit=None):
    args = [near(v) if spec == "near" else v for spec, v in zip(specs, args)]
    specs = [VMEM if spec == "near" else spec for spec in specs]
    single = not isinstance(outs, list)
    outs = [outs] if single else outs
    result = pl.pallas_call(
        kernel,
        out_shape=[pltpu.VMEM(shape, kind) for shape, kind in outs],
        in_specs=specs,
        out_specs=[VMEM] * len(outs),
        scratch_shapes=scratch,
        compiler_params=pltpu.CompilerParams(vmem_limit_bytes=limit),
    )(*args)
    return result[0] if single else result


def body(ham_blocks, ham_index, coef_blocks, coef_index, slab_blocks, slab_index, pattern_index):
    cores = [(i, i ^ 1) for i in range(COLS)]

    names = run(name_kernel, ((COLS, 8, 128), BF), [VMEM, VMEM], [slab_index, pattern_index])
    named = lax.all_to_all(names, "col", 0, 0)

    parts, turned = run(
        split_kernel,
        [((16, 8, 256), BF), ((4, 128, 128), BF)],
        [ANY, VMEM],
        [ham_blocks, coef_blocks],
        [pltpu.VMEM((8, 4, 16, 128), BF), pltpu.SemaphoreType.DMA],
    )
    swapped = lax.ppermute(slab_blocks[0, 0], "col", cores)

    stamped = run(stamp_kernel, ((16, 8, 384), BF), [SMEM, SMEM, "near", "near"], [ham_index, coef_index, named, parts])
    got = lax.all_to_all(stamped, "row", 0, 0)

    pair = jnp.stack([slab_blocks[0, 0], swapped])
    line = [pair] + [shift(pair, 0, d) for d in (1, 2, 3)]
    line = jnp.stack(line)
    slabs = [line, shift(line, 1, 0)]

    picked = run(pick_kernel, ((16, 16, 256), BF), ["near"], [got])
    picks = lax.all_to_all(picked, "row", 0, 0)

    numbers = got[:, 0, 256:384].astype(I32)
    ham_names = got[:, :, 256:260].reshape(128, 4).astype(I32)
    wanted = run(choose_kernel, ((16, 256, 128), BF), [SMEM, "near"], [numbers, turned], limit=LIMIT)
    wanted, picks = lax.optimization_barrier((wanted, picks))
    coefs = lax.all_to_all(wanted, "row", 0, 0)

    piece = run(pack_kernel, ((16, 16, 256), BF), ["near"], [picks], limit=LIMIT)
    across = shift(piece, 1, 0)
    hams = [piece, across]
    for d in (1, 3, 2):
        hams += [shift(piece, 0, d), shift(across, 0, d)]

    match = pl.pallas_call(
        match_kernel,
        out_shape=pltpu.SMEM((128,), I32),
        in_specs=[SMEM] * 2,
        out_specs=SMEM,
        scratch_shapes=[pltpu.SMEM((256,), I32)],
        compiler_params=pltpu.CompilerParams(vmem_limit_bytes=LIMIT),
        name="match",
    )(ham_names, numbers)
    match = pltpu.with_memory_space_constraint(match, pltpu.SMEM)

    ham = run(gather_kernel, ((16, 128, 256), BF), ["near"] * 8, hams, limit=LIMIT)
    across = lax.ppermute(ham, "col", cores)
    return pl.pallas_call(
        product_kernel,
        out_shape=jax.ShapeDtypeStruct((1, 2, 128, 128), BF),
        in_specs=[SMEM] + [VMEM] * 5,
        out_specs=VMEM,
        scratch_shapes=[pltpu.VMEM((8, 256, 256), BF), pltpu.VMEM((2, 2, 256, 256), BF)],
        compiler_params=pltpu.CompilerParams(vmem_limit_bytes=LIMIT),
        name="product",
    )(match, near(coefs), near(ham), near(across), near(slabs[0]), near(slabs[1]))


def solution(mesh):
    placed = (
        P("row", None, None, None),
        P("row", None),
        P("col", "row", None, None),
        P("col", "row"),
        P("row", "col", None, None),
        P("row", "col"),
        P("row", "col"),
    )
    return jax.shard_map(body, mesh=mesh, in_specs=placed, out_specs=P("row", "col", None, None), check_vma=False)
```

```python
import jax
import jax.numpy as jnp
from jax import lax
from jax.experimental import pallas as pl
from jax.experimental.pallas import tpu as pltpu
from jax.sharding import PartitionSpec as P


BF = jnp.bfloat16
F32 = jnp.float32
I32 = jnp.int32
COLS = 16
LIMIT = 16 << 20
PLACES = ((0, 0), (1, 0), (0, 1), (1, 1), (0, 3), (1, 3), (0, 2), (1, 2))
SMEM = pl.BlockSpec(memory_space=pltpu.SMEM)
VMEM = pl.BlockSpec(memory_space=pltpu.VMEM)
ANY = pl.BlockSpec(memory_space=pl.ANY)


def iota(shape, dim):
    return lax.broadcasted_iota(I32, shape, dim)


def hot(cond):
    return jnp.where(cond, 1.0, 0.0).astype(BF)


def dot(a, b):
    return jnp.dot(a, b, preferred_element_type=F32)


def name_kernel(slab_idx, pattern, send):
    lane = iota((8, 128), 1)
    line = jnp.where(lane == 0, slab_idx[0], jnp.where(lane == 1, pattern[0, 0], pattern[0, 1]))
    send[...] = jnp.broadcast_to(line.astype(F32).astype(BF)[None], send.shape)


def split_kernel(ham, coef, send, turned, part, sem):
    col = lax.axis_index("col")
    chip, core = col // 2, col % 2
    copy = pltpu.make_async_copy(ham.at[:, :, pl.ds(pl.multiple_of(chip * 16, 16), 16), :], part, sem)
    copy.start()
    for j in range(4):
        turned[j] = coef[j, 0].T
    a, b = iota((128, 128), 0), iota((128, 128), 1)
    order = hot((a // 8 == b % 16) & (a % 8 == b // 16))
    first = hot((b < 64) & (a == b + 64 * core))
    second = hot((b >= 64) & (a == b - 64 + 64 * core))
    copy.wait()
    for s in range(2):
        left = part[:, 2 * s].reshape(128, 128)
        right = part[:, 2 * s + 1].reshape(128, 128)
        half = (dot(left, first) + dot(right, second)).astype(BF)
        send[:, :, s * 128 : (s + 1) * 128] = dot(order, half).reshape(16, 8, 128).astype(BF)


def stamp_kernel(ham_idx, coef_idx, named, parts, send):
    send[:, :, 0:256] = parts[...]
    lane, line = iota((8, 128), 1), iota((8, 128), 0)
    meta = jnp.zeros((8, 128), I32)
    for p in range(8):
        for k in range(4):
            meta = jnp.where((line == p) & (lane == k), ham_idx[k, p], meta)
    for j in range(4):
        meta = jnp.where(lane == 4 + j, coef_idx[0, j], meta)
    a, b = iota((128, 128), 0), iota((128, 128), 1)
    flat = named[...].astype(F32).reshape(128, 128).astype(BF)
    slabs = (b >= 16) & (b < 32)
    pats = (b >= 32) & (b < 64)
    src = jnp.where(slabs, 0, 1 + b % 2)
    at = jnp.where(slabs, b - 16, (b - 32) // 2)
    picked = dot(flat, hot((slabs | pats) & (a == src)))
    line_all = jnp.sum(jnp.where(a == 8 * at, picked, 0.0), axis=0, keepdims=True)
    meta = meta.astype(F32) + line_all
    send[:, :, 256:384] = jnp.broadcast_to(meta.astype(BF)[None], (16, 8, 128))


def pick_kernel(got, send):
    pieces = got[:, :, 0:256].astype(F32).reshape(128, 256).astype(BF)
    flat = got[:, :, 256:384].astype(F32).reshape(128, 128).astype(BF)
    a, b = iota((16, 128), 0), iota((16, 128), 1)
    names = lax.dot_general(hot(b == 16 + a), flat, (((1,), (1,)), ((), ())), preferred_element_type=F32)
    lane = b.astype(F32)
    picks = jnp.concatenate(
        [jnp.where(names[:, 8 * r : 8 * r + 1] == lane, 1.0, 0.0) for r in range(16)], axis=0
    )
    send[...] = dot(picks.astype(BF), pieces).astype(BF).reshape(16, 16, 256)


def pack_kernel(got, piece):
    a, b = iota((256, 256), 0), iota((256, 256), 1)
    order = hot((a // 16 == b % 16) & (a % 16 == b // 16))
    piece[...] = dot(order, got[...].reshape(256, 256)).astype(BF).reshape(16, 16, 256)


def choose_kernel(tables, turned, send):
    col = lax.axis_index("col")
    for r in range(16):
        for e in range(2):
            send[r, 128 * e : 128 * e + 128] = turned[tables[r, 32 + 2 * col + e] - 4 * col]


def match_kernel(ham_names, tables, out, slots):
    row, col = lax.axis_index("row"), lax.axis_index("col")

    def clear(q, _):
        for i in range(32):
            slots[q * 32 + i] = -1
        return 0

    lax.fori_loop(0, 8, clear, 0)
    for e in range(2):
        base = 4 + tables[row, 32 + 2 * col + e] - 4 * col
        for m in range(16):
            slots[e * 128 + tables[m, base]] = m
    for m in range(16):
        p = tables[row, 16 + m]
        for k in range(4):
            q = ham_names[p, k]
            for e in range(2):
                out[m * 8 + k * 2 + e] = jnp.where(q >= 0, slots[e * 128 + jnp.maximum(q, 0)], -1)


def gather_kernel(*refs):
    hams, ham = refs[:8], refs[8]
    chip = lax.axis_index("col") // 2
    x, y = chip // 4, chip % 4
    for t, (dx, dy) in enumerate(PLACES):
        s = ((x + dx) % 2) * 4 + (y - dy + 4) % 4
        ham[:, pl.ds(pl.multiple_of(s * 16, 16), 16), :] = hams[t][...]


def slab_kernel(near_slabs, far_slabs, slab):
    col = lax.axis_index("col")
    chip, core = col // 2, col % 2
    x, y = chip // 4, chip % 4
    for s in range(8):
        d = (y - s % 4 + 4) % 4
        for h in range(2):
            at = (h + core) % 2
            slab[s, :, 128 * h : 128 * h + 128] = jnp.where(x == s // 4, near_slabs[d, at], far_slabs[d, at])


def hold_kernel(across, held):
    held[...] = across[...]


def product_kernel(match, coefs, ham, across, slab, out, image, chosen):
    core = lax.axis_index("col") % 2
    for m in range(16):
        for k in range(4):
            for e in range(2):
                slot = match[m * 8 + k * 2 + e]
                for h in range(2):
                    half = core if h == 0 else 1 - core
                    at = pl.ds(pl.multiple_of(128 * e + 64 * half, 64), 64)
                    found = coefs[jnp.maximum(slot, 0), at]
                    chosen[m % 2, h, k * 64 : k * 64 + 64, e * 128 : e * 128 + 128] = jnp.where(
                        slot >= 0, found, jnp.zeros_like(found)
                    )
        image[m // 2, 128 * (m % 2) : 128 * (m % 2) + 128] = (dot(ham[m], chosen[m % 2, 0]) + dot(across[m], chosen[m % 2, 1])).astype(BF)
    total = jnp.zeros((128, 256), F32)
    for s in range(8):
        total = total + dot(slab[s], image[s])
    for e in range(2):
        out[0, e] = total[:, e * 128 : e * 128 + 128].astype(BF)


def shift(value, dx, dy):
    pairs = [
        (x * 8 + y * 2 + k, ((x + dx) % 2) * 8 + ((y + dy) % 4) * 2 + k)
        for x in range(2)
        for y in range(4)
        for k in range(2)
    ]
    return lax.ppermute(value, "col", pairs)


def near(value):
    return pltpu.with_memory_space_constraint(value, pltpu.VMEM)


def run(kernel, outs, specs, args, scratch=(), limit=None):
    args = [near(v) if spec == "near" else v for spec, v in zip(specs, args)]
    specs = [VMEM if spec == "near" else spec for spec in specs]
    single = not isinstance(outs, list)
    outs = [outs] if single else outs
    result = pl.pallas_call(
        kernel,
        out_shape=[pltpu.VMEM(shape, kind) for shape, kind in outs],
        in_specs=specs,
        out_specs=[VMEM] * len(outs),
        scratch_shapes=scratch,
        compiler_params=pltpu.CompilerParams(vmem_limit_bytes=limit),
    )(*args)
    return result[0] if single else result


def body(ham_blocks, ham_index, coef_blocks, coef_index, slab_blocks, slab_index, pattern_index):
    cores = [(i, i ^ 1) for i in range(COLS)]

    names = run(name_kernel, ((COLS, 8, 128), BF), [SMEM, SMEM], [slab_index.reshape(1), pattern_index])
    named = lax.all_to_all(names, "col", 0, 0)

    parts, turned = run(
        split_kernel,
        [((16, 8, 256), BF), ((4, 128, 128), BF)],
        [ANY, VMEM],
        [ham_blocks, coef_blocks],
        [pltpu.VMEM((8, 4, 16, 128), BF), pltpu.SemaphoreType.DMA],
    )
    swapped = lax.ppermute(slab_blocks[0, 0], "col", cores)

    stamped = run(
        stamp_kernel,
        ((16, 8, 384), BF),
        [SMEM, SMEM, "near", "near"],
        [ham_index.T, coef_index.T, named, parts],
    )
    got = lax.all_to_all(stamped, "row", 0, 0)

    pair = jnp.stack([slab_blocks[0, 0], swapped])
    line = [pair] + [shift(pair, 0, d) for d in (1, 2, 3)]
    line = jnp.stack(line)
    slabs = [line, shift(line, 1, 0)]

    picked = run(pick_kernel, ((16, 16, 256), BF), ["near"], [got])
    picks = lax.all_to_all(picked, "row", 0, 0)

    numbers = got[:, 0, 256:384].astype(I32)
    ham_names = got[:, :, 256:260].reshape(128, 4).astype(I32)
    wanted = run(
        choose_kernel, ((16, 256, 128), BF), [SMEM, "near"], [numbers, turned], limit=LIMIT
    )
    wanted, picks = lax.optimization_barrier((wanted, picks))
    coefs = lax.all_to_all(wanted, "row", 0, 0)

    piece = run(pack_kernel, ((16, 16, 256), BF), ["near"], [picks], limit=LIMIT)
    across = shift(piece, 1, 0)
    hams = [piece, across]
    for d in (1, 3, 2):
        hams += [shift(piece, 0, d), shift(across, 0, d)]

    match = pl.pallas_call(
        match_kernel,
        out_shape=pltpu.SMEM((128,), I32),
        in_specs=[SMEM] * 2,
        out_specs=SMEM,
        scratch_shapes=[pltpu.SMEM((256,), I32)],
        compiler_params=pltpu.CompilerParams(vmem_limit_bytes=LIMIT),
        name="match",
    )(ham_names, numbers)
    match = pltpu.with_memory_space_constraint(match, pltpu.SMEM)

    ham = run(gather_kernel, ((16, 128, 256), BF), ["near"] * 8, hams, limit=LIMIT)
    across = lax.ppermute(ham, "col", cores)
    across = run(hold_kernel, ((16, 128, 256), BF), ["near"], [across], limit=LIMIT)
    slab = run(slab_kernel, ((8, 128, 256), BF), ["near", "near"], slabs, limit=LIMIT)
    return pl.pallas_call(
        product_kernel,
        out_shape=jax.ShapeDtypeStruct((1, 2, 128, 128), BF),
        in_specs=[SMEM] + [VMEM] * 4,
        out_specs=VMEM,
        scratch_shapes=[pltpu.VMEM((8, 256, 256), BF), pltpu.VMEM((2, 2, 256, 256), BF)],
        compiler_params=pltpu.CompilerParams(vmem_limit_bytes=LIMIT),
        name="product",
    )(match, near(coefs), near(ham), near(across), near(slab))


def solution(mesh):
    placed = (
        P("row", None, None, None),
        P("row", None),
        P("col", "row", None, None),
        P("col", "row"),
        P("row", "col", None, None),
        P("row", "col"),
        P("row", "col"),
    )
    return jax.shard_map(
        body, mesh=mesh, in_specs=placed, out_specs=P("row", "col", None, None), check_vma=False
    )
```

```python
import jax
import jax.numpy as jnp
from jax import lax
from jax.experimental import pallas as pl
from jax.experimental.pallas import tpu as pltpu
from jax.sharding import PartitionSpec as P


BF = jnp.bfloat16
F32 = jnp.float32
I32 = jnp.int32
COLS = 16
LIMIT = 16 << 20
PLACES = ((0, 0), (1, 0), (0, 1), (1, 1), (0, 3), (1, 3), (0, 2), (1, 2))
SMEM = pl.BlockSpec(memory_space=pltpu.SMEM)
VMEM = pl.BlockSpec(memory_space=pltpu.VMEM)
ANY = pl.BlockSpec(memory_space=pl.ANY)


def iota(shape, dim):
    return lax.broadcasted_iota(I32, shape, dim)


def hot(cond):
    return jnp.where(cond, 1.0, 0.0).astype(BF)


def dot(a, b):
    return jnp.dot(a, b, preferred_element_type=F32)


def name_kernel(slab_idx, pattern, send):
    lane = iota((8, 128), 1)
    line = jnp.where(lane == 0, slab_idx[0], jnp.where(lane == 1, pattern[0, 0], pattern[0, 1]))
    send[...] = jnp.broadcast_to(line.astype(F32).astype(BF)[None], send.shape)


def split_kernel(ham, coef, send, turned, part, sem):
    col = lax.axis_index("col")
    chip, core = col // 2, col % 2
    copy = pltpu.make_async_copy(ham.at[:, :, pl.ds(pl.multiple_of(chip * 16, 16), 16), :], part, sem)
    copy.start()
    for j in range(4):
        turned[j] = coef[j, 0].T
    a, b = iota((128, 128), 0), iota((128, 128), 1)
    order = hot((a // 8 == b % 16) & (a % 8 == b // 16))
    first = hot((b < 64) & (a == b + 64 * core))
    second = hot((b >= 64) & (a == b - 64 + 64 * core))
    copy.wait()
    for s in range(2):
        left = part[:, 2 * s].reshape(128, 128)
        right = part[:, 2 * s + 1].reshape(128, 128)
        half = (dot(left, first) + dot(right, second)).astype(BF)
        send[:, :, s * 128 : (s + 1) * 128] = dot(order, half).reshape(16, 8, 128).astype(BF)


def stamp_kernel(ham_idx, coef_idx, named, parts, send):
    send[:, :, 0:256] = parts[...]
    lane, line = iota((8, 128), 1), iota((8, 128), 0)
    meta = jnp.zeros((8, 128), I32)
    for p in range(8):
        for k in range(4):
            meta = jnp.where((line == p) & (lane == k), ham_idx[k, p], meta)
    for j in range(4):
        meta = jnp.where(lane == 4 + j, coef_idx[0, j], meta)
    a, b = iota((128, 128), 0), iota((128, 128), 1)
    flat = named[...].astype(F32).reshape(128, 128).astype(BF)
    slabs = (b >= 16) & (b < 32)
    pats = (b >= 32) & (b < 64)
    src = jnp.where(slabs, 0, 1 + b % 2)
    at = jnp.where(slabs, b - 16, (b - 32) // 2)
    picked = dot(flat, hot((slabs | pats) & (a == src)))
    line_all = jnp.sum(jnp.where(a == 8 * at, picked, 0.0), axis=0, keepdims=True)
    meta = meta.astype(F32) + line_all
    send[:, :, 256:384] = jnp.broadcast_to(meta.astype(BF)[None], (16, 8, 128))


def pick_kernel(got, send):
    pieces = got[:, :, 0:256].astype(F32).reshape(128, 256).astype(BF)
    flat = got[:, :, 256:384].astype(F32).reshape(128, 128).astype(BF)
    a, b = iota((16, 128), 0), iota((16, 128), 1)
    names = lax.dot_general(hot(b == 16 + a), flat, (((1,), (1,)), ((), ())), preferred_element_type=F32)
    lane = b.astype(F32)
    picks = jnp.concatenate(
        [jnp.where(names[:, 8 * r : 8 * r + 1] == lane, 1.0, 0.0) for r in range(16)], axis=0
    )
    send[...] = dot(picks.astype(BF), pieces).astype(BF).reshape(16, 16, 256)


def pack_kernel(got, piece):
    a, b = iota((256, 256), 0), iota((256, 256), 1)
    order = hot((a // 16 == b % 16) & (a % 16 == b // 16))
    piece[...] = dot(order, got[...].reshape(256, 256)).astype(BF).reshape(16, 16, 256)


def choose_kernel(tables, turned, send):
    col = lax.axis_index("col")
    for r in range(16):
        for e in range(2):
            send[r, 128 * e : 128 * e + 128] = turned[tables[r, 32 + 2 * col + e] - 4 * col]


def match_kernel(ham_names, tables, out, slots):
    row, col = lax.axis_index("row"), lax.axis_index("col")

    def clear(q, _):
        for i in range(32):
            slots[q * 32 + i] = -1
        return 0

    lax.fori_loop(0, 8, clear, 0)
    for e in range(2):
        base = 4 + tables[row, 32 + 2 * col + e] - 4 * col
        for m in range(16):
            slots[e * 128 + tables[m, base]] = m
    for m in range(16):
        p = tables[row, 16 + m]
        for k in range(4):
            q = ham_names[p, k]
            for e in range(2):
                out[m * 8 + k * 2 + e] = jnp.where(q >= 0, slots[e * 128 + jnp.maximum(q, 0)], -1)


def gather_kernel(*refs):
    hams, ham = refs[:8], refs[8]
    chip = lax.axis_index("col") // 2
    x, y = chip // 4, chip % 4
    for t, (dx, dy) in enumerate(PLACES):
        s = ((x + dx) % 2) * 4 + (y - dy + 4) % 4
        ham[:, pl.ds(pl.multiple_of(s * 16, 16), 16), :] = hams[t][...]


def slab_kernel(near_slabs, far_slabs, slab, last):
    col = lax.axis_index("col")
    chip, core = col // 2, col % 2
    x, y = chip // 4, chip % 4
    for s in range(8):
        d = (y - s % 4 + 4) % 4
        for h in range(2):
            at = (h + core) % 2
            block = jnp.where(x == s // 4, near_slabs[d, at], far_slabs[d, at])
            if s < 6:
                slab[s, :, 128 * h : 128 * h + 128] = block
            else:
                last[s - 6, :, 128 * h : 128 * h + 128] = block


def hold_kernel(across, held):
    held[...] = across[...]


def product_kernel(match, coefs, ham, across, slab, last, out, image, chosen):
    core = lax.axis_index("col") % 2
    for m in range(16):
        for k in range(4):
            for e in range(2):
                slot = match[m * 8 + k * 2 + e]
                for h in range(2):
                    half = core if h == 0 else 1 - core
                    at = pl.ds(pl.multiple_of(128 * e + 64 * half, 64), 64)
                    found = coefs[jnp.maximum(slot, 0), at]
                    chosen[m % 2, h, k * 64 : k * 64 + 64, e * 128 : e * 128 + 128] = jnp.where(
                        slot >= 0, found, jnp.zeros_like(found)
                    )
        image[m // 2, 128 * (m % 2) : 128 * (m % 2) + 128] = (dot(ham[m], chosen[m % 2, 0]) + dot(across[m], chosen[m % 2, 1])).astype(BF)
    total = jnp.zeros((128, 256), F32)
    for s in range(8):
        total = total + dot(slab[s] if s < 6 else last[s - 6], image[s])
    for e in range(2):
        out[0, e] = total[:, e * 128 : e * 128 + 128].astype(BF)


def shift(value, dx, dy):
    pairs = [
        (x * 8 + y * 2 + k, ((x + dx) % 2) * 8 + ((y + dy) % 4) * 2 + k)
        for x in range(2)
        for y in range(4)
        for k in range(2)
    ]
    return lax.ppermute(value, "col", pairs)


def near(value):
    return pltpu.with_memory_space_constraint(value, pltpu.VMEM)


def run(kernel, outs, specs, args, scratch=(), limit=None):
    args = [near(v) if spec == "near" else v for spec, v in zip(specs, args)]
    specs = [VMEM if spec == "near" else spec for spec in specs]
    single = not isinstance(outs, list)
    outs = [outs] if single else outs
    result = pl.pallas_call(
        kernel,
        out_shape=[pltpu.VMEM(shape, kind) for shape, kind in outs],
        in_specs=specs,
        out_specs=[VMEM] * len(outs),
        scratch_shapes=scratch,
        compiler_params=pltpu.CompilerParams(vmem_limit_bytes=limit),
    )(*args)
    return result[0] if single else result


def body(ham_blocks, ham_index, coef_blocks, coef_index, slab_blocks, slab_index, pattern_index):
    cores = [(i, i ^ 1) for i in range(COLS)]

    names = run(name_kernel, ((COLS, 8, 128), BF), [SMEM, SMEM], [slab_index.reshape(1), pattern_index])
    named = lax.all_to_all(names, "col", 0, 0)

    parts, turned = run(
        split_kernel,
        [((16, 8, 256), BF), ((4, 128, 128), BF)],
        [ANY, VMEM],
        [ham_blocks, coef_blocks],
        [pltpu.VMEM((8, 4, 16, 128), BF), pltpu.SemaphoreType.DMA],
    )
    swapped = lax.ppermute(slab_blocks[0, 0], "col", cores)

    stamped = run(
        stamp_kernel,
        ((16, 8, 384), BF),
        [SMEM, SMEM, "near", "near"],
        [ham_index.T, coef_index.T, named, parts],
    )
    got = lax.all_to_all(stamped, "row", 0, 0)

    pair = jnp.stack([slab_blocks[0, 0], swapped])
    line = [pair] + [shift(pair, 0, d) for d in (1, 2, 3)]
    line = jnp.stack(line)
    slabs = [line, shift(line, 1, 0)]

    picked = run(pick_kernel, ((16, 16, 256), BF), ["near"], [got])
    picks = lax.all_to_all(picked, "row", 0, 0)

    numbers = got[:, 0, 256:384].astype(I32)
    ham_names = got[:, :, 256:260].reshape(128, 4).astype(I32)
    wanted = run(
        choose_kernel, ((16, 256, 128), BF), [SMEM, "near"], [numbers, turned], limit=LIMIT
    )
    wanted, picks = lax.optimization_barrier((wanted, picks))
    coefs = lax.all_to_all(wanted, "row", 0, 0)

    piece = run(pack_kernel, ((16, 16, 256), BF), ["near"], [picks], limit=LIMIT)
    across = shift(piece, 1, 0)
    hams = [piece, across]
    for d in (1, 3, 2):
        hams += [shift(piece, 0, d), shift(across, 0, d)]

    match = pl.pallas_call(
        match_kernel,
        out_shape=pltpu.SMEM((128,), I32),
        in_specs=[SMEM] * 2,
        out_specs=SMEM,
        scratch_shapes=[pltpu.SMEM((256,), I32)],
        compiler_params=pltpu.CompilerParams(vmem_limit_bytes=LIMIT),
        name="match",
    )(ham_names, numbers)
    match = pltpu.with_memory_space_constraint(match, pltpu.SMEM)

    ham = run(gather_kernel, ((16, 128, 256), BF), ["near"] * 8, hams, limit=LIMIT)
    across = lax.ppermute(ham, "col", cores)
    across = run(hold_kernel, ((16, 128, 256), BF), ["near"], [across], limit=LIMIT)
    slab, last = run(slab_kernel, [((6, 128, 256), BF), ((2, 128, 256), BF)], ["near", "near"], slabs, limit=LIMIT)
    return pl.pallas_call(
        product_kernel,
        out_shape=jax.ShapeDtypeStruct((1, 2, 128, 128), BF),
        in_specs=[SMEM] + [VMEM] * 5,
        out_specs=VMEM,
        scratch_shapes=[pltpu.VMEM((8, 256, 256), BF), pltpu.VMEM((2, 2, 256, 256), BF)],
        compiler_params=pltpu.CompilerParams(vmem_limit_bytes=LIMIT),
        name="product",
    )(match, near(coefs), near(ham), near(across), near(slab), last)


def solution(mesh):
    placed = (
        P("row", None, None, None),
        P("row", None),
        P("col", "row", None, None),
        P("col", "row"),
        P("row", "col", None, None),
        P("row", "col"),
        P("row", "col"),
    )
    return jax.shard_map(
        body, mesh=mesh, in_specs=placed, out_specs=P("row", "col", None, None), check_vma=False
    )
```
